256 devices in a mesh: seq: 64 (over y, x, z_hi, core), chan: 4 (over z_lo).
Axes of the slice: x: 4, y: 4, z: 8 (z_hi: 2, z_lo: 4; z = z_hi * 4 + z_lo), core: 2. Of those that a mesh axis runs over, the one named last changes fastest.
Arguments:
- tokens: bfloat16 [512, 768, 1024], P('seq', 'chan'), may hold values from -24 to 24, as said below
- filter_gain: bfloat16 [512, 768, 1024], P('seq', 'chan'), may hold values from -4 to 4
- row_factor: bfloat16 [1024, 1024], replicated, may hold values from -0.1875 to 0.1875
- col_factor: bfloat16 [512, 512], replicated, may hold values from -0.25 to 0.25
- up_weight: bfloat16 [4, 192, 768], P('chan'), may hold values from -0.4375 to 0.4375
- down_weight: bfloat16 [4, 192, 768], P('chan'), may hold values from -0.21875 to 0.21875
Outputs:
- layer_out: bfloat16 [512, 768, 1024], P('seq', 'chan')
The draws below stay inside these ranges and needn't reach their ends.
Inputs may be any that keep to these rules, and one draw needn't show every extreme that they name: `tokens`: layer activations.
All inputs are finite; a program needn't handle non-finite values.
Results may differ from the reference program's by a relative error of at most 0.0075.
Values may be sent and summed in bfloat16 or wider, within the bound.
A program may use at most 128 MiB of HBM per device.

```python
import math
import jax
import jax.numpy as jnp
from jax import lax

GA = 512
GB = 1024
D = 768
BLOCKS = 4
BW = 192
HB = 768


def draw_tokens(key, part):
    base_key = jax.random.fold_in(key, 11)
    scale_key = jax.random.fold_in(key, 23)
    channel = jnp.arange(D, dtype=jnp.float32)
    chan_scale = (0.3 * 10.0 ** (channel / (D - 1))).reshape(1, D, 1)
    tok_scale = jnp.exp(jax.random.uniform(scale_key, (GA, 1, GB), jnp.float32, math.log(0.5), math.log(2.0)))
    base = jnp.clip(jax.random.normal(base_key, (GA, D, GB), jnp.float32), -4.0, 4.0)
    return (base * chan_scale * tok_scale).astype(jnp.bfloat16)


def block_scale(stream_key, extent, shards, low, largest):
    level = 1.0
    for position, blocks in shards:
        heights = jax.random.uniform(jax.random.fold_in(jax.random.fold_in(stream_key, 6), position), (blocks,), jnp.float32, low / len(shards), largest / len(shards))
        level = level * jnp.repeat(jnp.exp(heights), extent[position] // blocks).reshape((-1,) + (1,) * (len(extent) - 1 - position))
    return level


def gaussian(own_key, dims, scale, bound, split=(), kind=jnp.bfloat16):
    entries = scale * jax.random.normal(own_key, dims, jnp.float32)
    if split:
        entries = entries * block_scale(own_key, dims, split, -0.22, 0.18)
    return jnp.clip(entries, -bound, bound).astype(kind)


def setup_inputs(seed: int = 0) -> dict:
    keys = jax.random.split(jax.random.key(seed), 7)
    tokens = draw_tokens(jax.random.fold_in(keys[6], 71), 0)
    filter_gain = gaussian(keys[1], (GA, D, GB), 1.0, 4.0, ((0, 64), (1, 4)))
    row_factor = gaussian(keys[2], (GB, GB), GB ** -0.5, 0.1875)
    col_factor = gaussian(keys[3], (GA, GA), GA ** -0.5, 0.25)
    up_weight = gaussian(keys[4], (BLOCKS, BW, HB), BW ** -0.5, 0.4375, ((0, 4),))
    down_weight = gaussian(keys[5], (BLOCKS, BW, HB), HB ** -0.5, 0.21875, ((0, 4),))
    return {"tokens": tokens, "filter_gain": filter_gain, "row_factor": row_factor, "col_factor": col_factor, "up_weight": up_weight, "down_weight": down_weight}


def reference(tokens, filter_gain, row_factor, col_factor, up_weight, down_weight):
    width = D // BLOCKS
    row_f = row_factor.astype(jnp.float32)
    col_f = col_factor.astype(jnp.float32)
    pieces = []
    for blk in range(BLOCKS):
        part = tokens[:, blk * width:(blk + 1) * width, :].astype(jnp.float32)
        spun = jnp.einsum('bk,ack->acb', row_f, part)
        gain = filter_gain[:, blk * width:(blk + 1) * width, :].astype(jnp.float32)
        filtered = (gain * spun).astype(jnp.bfloat16)
        mixed = jnp.einsum('ak,kcb->acb', col_f, filtered.astype(jnp.float32))
        pieces.append(mixed.astype(jnp.bfloat16))
    mixed_all = jnp.concatenate(pieces, axis=1)
    up_f = up_weight.astype(jnp.float32)
    down_f = down_weight.astype(jnp.float32)

    def finish(pair):
        source, mixed_row = pair
        src = source.astype(jnp.float32)
        gated = src + mixed_row.astype(jnp.float32) * jax.nn.sigmoid(src)
        mean = lax.optimization_barrier(jnp.mean(gated, axis=0, keepdims=True))
        centered = gated - mean
        spread = lax.optimization_barrier(jnp.mean(centered * centered, axis=0, keepdims=True))
        normed = (centered * lax.rsqrt(spread + 1e-05)).astype(jnp.bfloat16)
        flat = normed.reshape(BLOCKS, width, GB).astype(jnp.float32)
        hidden = jax.nn.gelu(jnp.einsum('nkt,nkh->nht', flat, up_f)).astype(jnp.bfloat16)
        back = jnp.einsum('nht,nkh->nkt', hidden.astype(jnp.float32), down_f)
        return (gated + back.reshape(D, GB)).astype(jnp.bfloat16)
    return lax.map(finish, (tokens, mixed_all))
```

```python
import jax
import jax.numpy as jnp
from jax import lax
from jax.sharding import PartitionSpec as P

D = 768


def finish(source, mixed, up_weight, down_weight):
    src = source.astype(jnp.float32)
    gated = src + mixed.astype(jnp.float32) * jax.nn.sigmoid(src)
    total = lax.psum(jnp.sum(gated, axis=1), "chan")
    mean = total / D
    centered = gated - mean[:, None, :]
    spread = lax.psum(jnp.sum(centered * centered, axis=1), "chan") / D
    normed = (centered * lax.rsqrt(spread + 1e-05)[:, None, :]).astype(jnp.bfloat16)
    hidden = jax.nn.gelu(
        jnp.einsum("xky,kh->xhy", normed, up_weight[0], preferred_element_type=jnp.float32)
    ).astype(jnp.bfloat16)
    back = jnp.einsum("xhy,kh->xky", hidden, down_weight[0], preferred_element_type=jnp.float32)
    return (gated + back).astype(jnp.bfloat16)


def body(tokens, filter_gain, row_factor, col_factor, up_weight, down_weight):
    spun = jnp.einsum("rck,bk->rcb", tokens, row_factor, preferred_element_type=jnp.float32)
    filtered = (filter_gain.astype(jnp.float32) * spun).astype(jnp.bfloat16)
    by_channel = jnp.transpose(filtered, (1, 0, 2))
    owned = lax.all_to_all(by_channel, "seq", split_axis=0, concat_axis=1, tiled=True)
    mixed = jnp.einsum("ak,ckb->cab", col_factor, owned, preferred_element_type=jnp.float32)
    back = lax.all_to_all(mixed.astype(jnp.bfloat16), "seq", split_axis=1, concat_axis=0, tiled=True)
    return finish(tokens, jnp.transpose(back, (1, 0, 2)), up_weight, down_weight)


def solution(mesh):
    return jax.shard_map(
        body,
        mesh=mesh,
        in_specs=(
            P("seq", "chan", None),
            P("seq", "chan", None),
            P(),
            P(),
            P("chan", None, None),
            P("chan", None, None),
        ),
        out_specs=P("seq", "chan", None),
        check_vma=False,
    )
```

```python
import jax
import jax.numpy as jnp
from jax import lax
from jax.experimental import pallas as pl
from jax.experimental.pallas import tpu as pltpu
from jax.sharding import PartitionSpec as P

ROWS = 8
CH = 192
COLS = 1024
HID = 768
D = 768
PEERS = 64
PARTS = 4
W = 128
NCH = COLS // W
OWN = CH // PEERS
GA = ROWS * PEERS
MESH = pl.DeviceIdType.MESH
F32 = jnp.float32
BF16 = jnp.bfloat16


def peer(me, i):
    y, x, z, c = me // 16, (me // 4) % 4, (me // 2) % 2, me % 2
    y = (y + i // 16) % 4
    x = (x + (i // 4) % 4) % 4
    z = (z + (i // 2) % 2) % 2
    c = (c + i % 2) % 2
    return ((y * 4 + x) * 2 + z) * 2 + c


def loop(lo, hi, f):
    def step(i, carry):
        f(i)
        return carry

    lax.fori_loop(lo, hi, step, 0)


def layer_kernel(
    tok_hbm, gain_hbm, rf_hbm, cf_hbm, up_hbm, down_hbm, out_hbm,
    tok, gain, rf, cf, up, down, filt, recv, mix, back, gated, stat, result,
    in_sem, rf_sem, gain_sem, fs_sem, fr_sem, bs_sem, br_sem, ss_sem, sr_sem, out_sem,
):
    me = lax.axis_index("seq")
    part = lax.axis_index("chan")

    def cols(j):
        return pl.ds(pl.multiple_of(j * W, W), W)

    def rf_copy(j):
        return pltpu.make_async_copy(rf_hbm.at[cols(j)], rf.at[cols(j)], rf_sem.at[j])

    def gain_copy(j):
        return pltpu.make_async_copy(gain_hbm.at[:, :, cols(j)], gain.at[j], gain_sem.at[j])

    tok_copy = pltpu.make_async_copy(tok_hbm, tok, in_sem.at[0])
    weights = [
        pltpu.make_async_copy(cf_hbm, cf, in_sem.at[1]),
        pltpu.make_async_copy(up_hbm, up, in_sem.at[2]),
        pltpu.make_async_copy(down_hbm, down, in_sem.at[3]),
    ]
    tok_copy.start()

    def start_chunk(j):
        rf_copy(j).start()
        gain_copy(j).start()

    loop(0, NCH, start_chunk)
    for copy in weights:
        copy.start()

    barrier = pltpu.get_barrier_semaphore()

    def greet(i):
        pl.semaphore_signal(barrier, inc=1, device_id=(peer(me, i), part), device_id_type=MESH)

    loop(1, PEERS, greet)
    for i in range(1, PARTS):
        pl.semaphore_signal(barrier, inc=1, device_id=(me, (part + i) % PARTS), device_id_type=MESH)

    i0 = lax.broadcasted_iota(jnp.int32, (128, 128), 0)
    i1 = lax.broadcasted_iota(jnp.int32, (128, 128), 1)
    to_chan = jnp.where(i1 == (i0 % 8) * 16 + i0 // 8, 1.0, 0.0).astype(BF16)
    to_rows = jnp.where(i1 == (i0 % 16) * 8 + i0 // 16, 1.0, 0.0).astype(BF16)
    filt_rows = filt.reshape(NCH * CH * ROWS, W)
    back_rows = back.reshape(NCH * CH * ROWS, W)

    def block(j, c):
        return pl.ds(pl.multiple_of(j * (CH * ROWS) + c * ROWS, 128), 128)

    def row_mix(j):
        rf_copy(j).wait()
        gain_copy(j).wait()
        for c0 in range(0, CH, 64):
            lhs = tok[:, c0 : c0 + 64, :].reshape(ROWS * 64, COLS)
            spun = lax.dot_general(lhs, rf[cols(j), :], (((1,), (1,)), ((), ())), preferred_element_type=F32)
            spun = spun.reshape(ROWS, 64, W)
            own = (gain[j, :, c0 : c0 + 64, :].astype(F32) * spun).astype(BF16)
            for c in range(0, 64, 16):
                piece = own[:, c : c + 16, :].reshape(128, W)
                filt_rows[block(j, c0 + c), :] = jnp.dot(to_chan, piece, preferred_element_type=F32).astype(BF16)

    def my_rows(d):
        return pl.ds(pl.multiple_of(d * ROWS, ROWS), ROWS)

    def send_filtered(j):
        def one(i):
            d = peer(me, i)
            pltpu.make_async_remote_copy(
                src_ref=filt.at[j, pl.ds(OWN * d, OWN)],
                dst_ref=recv.at[j, :, my_rows(me), :],
                send_sem=fs_sem.at[j],
                recv_sem=fr_sem.at[j],
                device_id=(d, part),
                device_id_type=MESH,
            ).start()

        loop(1, PEERS, one)
        pltpu.make_async_copy(filt.at[j, pl.ds(OWN * me, OWN)], recv.at[j, :, my_rows(me), :], fr_sem.at[j]).start()

    def col_mix(j):
        pltpu.make_async_copy(recv.at[j], recv.at[j], fr_sem.at[j]).wait()
        rhs = jnp.concatenate([recv[j, c] for c in range(OWN)], axis=1)
        mixed = jnp.dot(cf[...], rhs, preferred_element_type=F32).astype(BF16)
        for c in range(OWN):
            mix[j, c] = mixed[:, c * W : (c + 1) * W]

    def send_mixed(j):
        def one(i):
            d = peer(me, i)
            pltpu.make_async_remote_copy(
                src_ref=mix.at[j, :, my_rows(d), :],
                dst_ref=back.at[j, pl.ds(OWN * me, OWN)],
                send_sem=bs_sem.at[j],
                recv_sem=br_sem.at[j],
                device_id=(d, part),
                device_id_type=MESH,
            ).start()

        loop(1, PEERS, one)
        pltpu.make_async_copy(mix.at[j, :, my_rows(me), :], back.at[j, pl.ds(OWN * me, OWN)], br_sem.at[j]).start()

    def gate(j):
        pltpu.make_async_copy(back.at[j], back.at[j], br_sem.at[j]).wait()
        slot = j % 2
        total = jnp.zeros((ROWS, W), F32)
        for c in range(0, CH, 16):
            mixed = jnp.dot(to_rows, back_rows[block(j, c), :], preferred_element_type=F32).reshape(ROWS, 16, W)
            src = tok[:, c : c + 16, cols(j)].astype(F32)
            value = src + mixed * jax.nn.sigmoid(src)
            gated[slot, :, c : c + 16, :] = value
            total = total + jnp.sum(value, axis=1)
        mean = total * (1.0 / CH)
        squares = jnp.zeros((ROWS, W), F32)
        for c in range(0, CH, 16):
            off = gated[slot, :, c : c + 16, :] - mean[:, None, :]
            squares = squares + jnp.sum(off * off, axis=1)
        stat[j, part, 0] = total
        stat[j, part, 1] = squares
        for i in range(1, PARTS):
            pltpu.make_async_remote_copy(
                src_ref=stat.at[j, part],
                dst_ref=stat.at[j, part],
                send_sem=ss_sem.at[j],
                recv_sem=sr_sem.at[j],
                device_id=(me, (part + i) % PARTS),
                device_id_type=MESH,
            ).start()

    def out_copy(j):
        return pltpu.make_async_copy(result.at[j], out_hbm.at[:, :, cols(j)], out_sem.at[j])

    def channel_mlp(j):
        three = stat.at[j, pl.ds(0, PARTS - 1)]
        pltpu.make_async_copy(three, three, sr_sem.at[j]).wait()
        slot = j % 2
        totals = [stat[j, p, 0] for p in range(PARTS)]
        mean = (totals[0] + totals[1] + totals[2] + totals[3]) * (1.0 / D)
        spread = jnp.zeros((ROWS, W), F32)
        for p in range(PARTS):
            off = totals[p] * (1.0 / CH) - mean
            spread = spread + (stat[j, p, 1] + CH * (off * off))
        scale = lax.rsqrt(spread * (1.0 / D) + 1e-05)
        for r0 in range(0, ROWS, 2):
            value = jnp.concatenate([gated[slot, r] for r in (r0, r0 + 1)], axis=1)
            m = jnp.concatenate([mean[r : r + 1] for r in (r0, r0 + 1)], axis=1)
            s = jnp.concatenate([scale[r : r + 1] for r in (r0, r0 + 1)], axis=1)
            normed = ((value - m) * s).astype(BF16)
            hidden = jax.nn.gelu(jnp.dot(up[...], normed, preferred_element_type=F32)).astype(BF16)
            final = (value + jnp.dot(down[...], hidden, preferred_element_type=F32)).astype(BF16)
            result[j, r0] = final[:, :W]
            result[j, r0 + 1] = final[:, W:]
        out_copy(j).start()

    tok_copy.wait()

    def first(j):
        row_mix(j)

        @pl.when(j == 0)
        def _():
            pl.semaphore_wait(barrier, PEERS - 1 + PARTS - 1)

        send_filtered(j)

    loop(0, NCH, first)
    for copy in weights:
        copy.wait()

    def second(j):
        col_mix(j)
        send_mixed(j)

    loop(0, NCH, second)
    gate(0)

    def third(j):
        gate(j)
        channel_mlp(j - 1)

    loop(1, NCH, third)
    channel_mlp(NCH - 1)

    def drain(j):
        rest = filt.at[j, pl.ds(0, CH - OWN)]
        pltpu.make_async_copy(rest, rest, fs_sem.at[j]).wait()
        pltpu.make_async_copy(rest, rest, bs_sem.at[j]).wait()
        three = stat.at[j, pl.ds(0, PARTS - 1)]
        pltpu.make_async_copy(three, three, ss_sem.at[j]).wait()
        out_copy(j).wait()

    loop(0, NCH, drain)


def body(tokens, filter_gain, row_factor, col_factor, up_weight, down_weight):
    dma = pltpu.SemaphoreType.DMA
    return pl.pallas_call(
        layer_kernel,
        name="mixer_layer",
        out_shape=jax.ShapeDtypeStruct((ROWS, CH, COLS), BF16),
        in_specs=[pl.BlockSpec(memory_space=pl.ANY)] * 6,
        out_specs=pl.BlockSpec(memory_space=pl.ANY),
        scratch_shapes=[
            pltpu.VMEM((ROWS, CH, COLS), BF16),
            pltpu.VMEM((NCH, ROWS, CH, W), BF16),
            pltpu.VMEM((COLS, COLS), BF16),
            pltpu.VMEM((GA, GA), BF16),
            pltpu.VMEM((HID, CH), BF16),
            pltpu.VMEM((CH, HID), BF16),
            pltpu.VMEM((NCH, CH, ROWS, W), BF16),
            pltpu.VMEM((NCH, OWN, GA, W), BF16),
            pltpu.VMEM((NCH, OWN, GA, W), BF16),
            pltpu.VMEM((NCH, CH, ROWS, W), BF16),
            pltpu.VMEM((2, ROWS, CH, W), F32),
            pltpu.VMEM((NCH, PARTS, 2, ROWS, W), F32),
            pltpu.VMEM((NCH, ROWS, CH, W), BF16),
            dma((4,)),
        ]
        + [dma((NCH,))] * 9,
        compiler_params=pltpu.CompilerParams(
            collective_id=0, has_side_effects=True, vmem_limit_bytes=60 * 2**20
        ),
    )(tokens, filter_gain, row_factor, col_factor, up_weight[0].T, down_weight[0])


def solution(mesh):
    return jax.shard_map(
        body,
        mesh=mesh,
        in_specs=(
            P("seq", "chan", None),
            P("seq", "chan", None),
            P(),
            P(),
            P("chan", None, None),
            P("chan", None, None),
        ),
        out_specs=P("seq", "chan", None),
        check_vma=False,
    )
```

```python
import jax
import jax.numpy as jnp
from jax import lax
from jax.experimental import pallas as pl
from jax.experimental.pallas import tpu as pltpu
from jax.sharding import PartitionSpec as P

ROWS = 8
CH = 192
COLS = 1024
HID = 768
D = 768
PEERS = 64
PARTS = 4
W = 128
NCH = COLS // W
OWN = CH // PEERS
PLANES = 4
PLANE = PEERS // PLANES
PCH = PLANE * OWN
GA = ROWS * PEERS
MESH = pl.DeviceIdType.MESH
F32 = jnp.float32
BF16 = jnp.bfloat16


def peer(me, i):
    y, x, z, c = me // 16, (me // 4) % 4, (me // 2) % 2, me % 2
    y = (y + i // 16) % 4
    x = (x + (i // 4) % 4) % 4
    z = (z + (i // 2) % 2) % 2
    c = (c + i % 2) % 2
    return ((y * 4 + x) * 2 + z) * 2 + c


def loop(lo, hi, f):
    def step(i, carry):
        f(i)
        return carry

    lax.fori_loop(lo, hi, step, 0)


def layer_kernel(
    tok_hbm, gain_hbm, rf_hbm, cf_hbm, up_hbm, down_hbm, out_hbm,
    tok, gain, rf, cf, up, down, up_t, filt, recv, mix, back, gated, stat, result,
    in_sem, rf_sem, gain_sem, fs_sem, fr_sem, bs_sem, br_sem, ss_sem, sr_sem, out_sem,
):
    me = lax.axis_index("seq")
    part = lax.axis_index("chan")

    def cols(j):
        return pl.ds(pl.multiple_of(j * W, W), W)

    def rf_copy(j):
        return pltpu.make_async_copy(rf_hbm.at[cols(j)], rf.at[cols(j)], rf_sem.at[j])

    def gain_copy(j):
        return pltpu.make_async_copy(gain_hbm.at[:, :, cols(j)], gain.at[j], gain_sem.at[j])

    def tok_copy(r):
        return pltpu.make_async_copy(tok_hbm.at[r], tok.at[r], in_sem.at[0])

    weights = [
        pltpu.make_async_copy(cf_hbm, cf, in_sem.at[1]),
        pltpu.make_async_copy(up_hbm, up, in_sem.at[2]),
        pltpu.make_async_copy(down_hbm, down, in_sem.at[3]),
    ]
    loop(0, ROWS, lambda r: tok_copy(r).start())

    def start_chunk(j):
        rf_copy(j).start()
        gain_copy(j).start()

    start_chunk(0)

    barrier = pltpu.get_barrier_semaphore()

    def greet(i):
        pl.semaphore_signal(barrier, inc=1, device_id=(peer(me, i), part), device_id_type=MESH)

    loop(1, PEERS, greet)
    for i in range(1, PARTS):
        pl.semaphore_signal(barrier, inc=1, device_id=(me, (part + i) % PARTS), device_id_type=MESH)

    i0 = lax.broadcasted_iota(jnp.int32, (128, 128), 0)
    i1 = lax.broadcasted_iota(jnp.int32, (128, 128), 1)
    to_chan = jnp.where(i1 == (i0 % 8) * 16 + i0 // 8, 1.0, 0.0).astype(BF16)
    to_rows = jnp.where(i1 == (i0 % 16) * 8 + i0 // 16, 1.0, 0.0).astype(BF16)
    filt_rows = filt.reshape(NCH * CH * ROWS, W)
    back_rows = back.reshape(NCH * CH * ROWS, W)

    def block(j, c):
        return pl.ds(pl.multiple_of(j * (CH * ROWS) + c * ROWS, 128), 128)

    def row_mix(j, plane):
        c0 = pl.multiple_of(plane * PCH, 16)
        lhs = tok[:, pl.ds(c0, PCH), :].reshape(ROWS * PCH, COLS)
        spun = lax.dot_general(lhs, rf[cols(j), :], (((1,), (1,)), ((), ())), preferred_element_type=F32)
        spun = spun.reshape(ROWS, PCH, W)
        own = (gain[j, :, pl.ds(c0, PCH), :].astype(F32) * spun).astype(BF16)
        for c in range(0, PCH, 16):
            piece = own[:, c : c + 16, :].reshape(128, W)
            filt_rows[block(j, c0 + c), :] = jnp.dot(to_chan, piece, preferred_element_type=F32).astype(BF16)

    def my_rows(d):
        return pl.ds(pl.multiple_of(d * ROWS, ROWS), ROWS)

    def send_filtered(j, lo, hi):
        def one(i):
            d = peer(me, i)
            pltpu.make_async_remote_copy(
                src_ref=filt.at[j, pl.ds(OWN * d, OWN)],
                dst_ref=recv.at[j, :, my_rows(me), :],
                send_sem=fs_sem.at[j],
                recv_sem=fr_sem.at[j],
                device_id=(d, part),
                device_id_type=MESH,
            ).start()

        loop(lo, hi, one)

    def keep_filtered(j):
        pltpu.make_async_copy(filt.at[j, pl.ds(OWN * me, OWN)], recv.at[j, :, my_rows(me), :], fr_sem.at[j]).start()

    def col_mix(j):
        pltpu.make_async_copy(recv.at[j], recv.at[j], fr_sem.at[j]).wait()
        rhs = jnp.concatenate([recv[j, c] for c in range(OWN)], axis=1)
        mixed = jnp.dot(cf[...], rhs, preferred_element_type=F32).astype(BF16)
        for c in range(OWN):
            mix[j, c] = mixed[:, c * W : (c + 1) * W]

    def send_mixed(j):
        def one(i):
            d = peer(me, i)
            pltpu.make_async_remote_copy(
                src_ref=mix.at[j, :, my_rows(d), :],
                dst_ref=back.at[j, pl.ds(OWN * me, OWN)],
                send_sem=bs_sem.at[j],
                recv_sem=br_sem.at[j],
                device_id=(d, part),
                device_id_type=MESH,
            ).start()

        loop(1, PEERS, one)
        pltpu.make_async_copy(mix.at[j, :, my_rows(me), :], back.at[j, pl.ds(OWN * me, OWN)], br_sem.at[j]).start()

    def gate(j):
        pltpu.make_async_copy(back.at[j], back.at[j], br_sem.at[j]).wait()
        slot = j % 2
        total = jnp.zeros((ROWS, W), F32)
        for c in range(0, CH, 16):
            mixed = jnp.dot(to_rows, back_rows[block(j, c), :], preferred_element_type=F32).reshape(ROWS, 16, W)
            src = tok[:, c : c + 16, cols(j)].astype(F32)
            value = src + mixed * jax.nn.sigmoid(src)
            gated[slot, :, c : c + 16, :] = value
            total = total + jnp.sum(value, axis=1)
        mean = total * (1.0 / CH)
        squares = jnp.zeros((ROWS, W), F32)
        for c in range(0, CH, 16):
            off = gated[slot, :, c : c + 16, :] - mean[:, None, :]
            squares = squares + jnp.sum(off * off, axis=1)
        stat[j, part, 0] = total
        stat[j, part, 1] = squares
        for i in range(1, PARTS):
            pltpu.make_async_remote_copy(
                src_ref=stat.at[j, part],
                dst_ref=stat.at[j, part],
                send_sem=ss_sem.at[j],
                recv_sem=sr_sem.at[j],
                device_id=(me, (part + i) % PARTS),
                device_id_type=MESH,
            ).start()

    def out_copy(j):
        return pltpu.make_async_copy(result.at[j], out_hbm.at[:, :, cols(j)], out_sem.at[j])

    def channel_mlp(j):
        three = stat.at[j, pl.ds(0, PARTS - 1)]
        pltpu.make_async_copy(three, three, sr_sem.at[j]).wait()
        slot = j % 2
        totals = [stat[j, p, 0] for p in range(PARTS)]
        mean = (totals[0] + totals[1] + totals[2] + totals[3]) * (1.0 / D)
        spread = jnp.zeros((ROWS, W), F32)
        for p in range(PARTS):
            off = totals[p] * (1.0 / CH) - mean
            spread = spread + (stat[j, p, 1] + CH * (off * off))
        scale = lax.rsqrt(spread * (1.0 / D) + 1e-05)
        for r0 in range(0, ROWS, 2):
            value = jnp.concatenate([gated[slot, r] for r in (r0, r0 + 1)], axis=1)
            m = jnp.concatenate([mean[r : r + 1] for r in (r0, r0 + 1)], axis=1)
            s = jnp.concatenate([scale[r : r + 1] for r in (r0, r0 + 1)], axis=1)
            normed = ((value - m) * s).astype(BF16)
            hidden = jax.nn.gelu(jnp.dot(up_t[...], normed, preferred_element_type=F32)).astype(BF16)
            final = (value + jnp.dot(down[...], hidden, preferred_element_type=F32)).astype(BF16)
            result[j, r0] = final[:, :W]
            result[j, r0 + 1] = final[:, W:]
        out_copy(j).start()

    pltpu.make_async_copy(tok_hbm, tok, in_sem.at[0]).wait()

    def plane_of(step):
        return (me // PLANE + step) % PLANES

    def first(j):
        rf_copy(j).wait()
        gain_copy(j).wait()
        row_mix(j, plane_of(0))

        @pl.when(j == 0)
        def _():
            pl.semaphore_wait(barrier, PEERS - 1 + PARTS - 1)
            loop(1, NCH, start_chunk)
            for copy in weights:
                copy.start()

        send_filtered(j, 1, PLANE)
        keep_filtered(j)

        def later(step):
            row_mix(j, plane_of(step))
            send_filtered(j, step * PLANE, step * PLANE + PLANE)

        loop(1, PLANES, later)

    loop(0, NCH, first)
    for copy in weights:
        copy.wait()
    up_t[...] = up[...].astype(F32).T.astype(BF16)

    def second(j):
        col_mix(j)
        send_mixed(j)

    loop(0, NCH, second)
    gate(0)

    def third(j):
        gate(j)
        channel_mlp(j - 1)

    loop(1, NCH, third)
    channel_mlp(NCH - 1)

    def drain(j):
        rest = filt.at[j, pl.ds(0, CH - OWN)]
        pltpu.make_async_copy(rest, rest, fs_sem.at[j]).wait()
        pltpu.make_async_copy(rest, rest, bs_sem.at[j]).wait()
        three = stat.at[j, pl.ds(0, PARTS - 1)]
        pltpu.make_async_copy(three, three, ss_sem.at[j]).wait()
        out_copy(j).wait()

    loop(0, NCH, drain)


def body(tokens, filter_gain, row_factor, col_factor, up_weight, down_weight):
    dma = pltpu.SemaphoreType.DMA
    return pl.pallas_call(
        layer_kernel,
        name="mixer_layer",
        out_shape=jax.ShapeDtypeStruct((ROWS, CH, COLS), BF16),
        in_specs=[pl.BlockSpec(memory_space=pl.ANY)] * 6,
        out_specs=pl.BlockSpec(memory_space=pl.ANY),
        scratch_shapes=[
            pltpu.VMEM((ROWS, CH, COLS), BF16),
            pltpu.VMEM((NCH, ROWS, CH, W), BF16),
            pltpu.VMEM((COLS, COLS), BF16),
            pltpu.VMEM((GA, GA), BF16),
            pltpu.VMEM((CH, HID), BF16),
            pltpu.VMEM((CH, HID), BF16),
            pltpu.VMEM((HID, CH), BF16),
            pltpu.VMEM((NCH, CH, ROWS, W), BF16),
            pltpu.VMEM((NCH, OWN, GA, W), BF16),
            pltpu.VMEM((NCH, OWN, GA, W), BF16),
            pltpu.VMEM((NCH, CH, ROWS, W), BF16),
            pltpu.VMEM((2, ROWS, CH, W), F32),
            pltpu.VMEM((NCH, PARTS, 2, ROWS, W), F32),
            pltpu.VMEM((NCH, ROWS, CH, W), BF16),
            dma((4,)),
        ]
        + [dma((NCH,))] * 9,
        compiler_params=pltpu.CompilerParams(
            collective_id=0, has_side_effects=True, vmem_limit_bytes=60 * 2**20
        ),
    )(tokens, filter_gain, row_factor, col_factor, up_weight[0], down_weight[0])


def solution(mesh):
    return jax.shard_map(
        body,
        mesh=mesh,
        in_specs=(
            P("seq", "chan", None),
            P("seq", "chan", None),
            P(),
            P(),
            P("chan", None, None),
            P("chan", None, None),
        ),
        out_specs=P("seq", "chan", None),
        check_vma=False,
    )
```

```python
import jax
import jax.numpy as jnp
from jax import lax
from jax.experimental import pallas as pl
from jax.experimental.pallas import tpu as pltpu
from jax.sharding import PartitionSpec as P

ROWS = 8
CH = 192
COLS = 1024
HID = 768
D = 768
PEERS = 64
PARTS = 4
W = 128
NCH = COLS // W
OWN = CH // PEERS
PLANES = 4
PLANE = PEERS // PLANES
PCH = PLANE * OWN
GA = ROWS * PEERS
LAG = 3
MESH = pl.DeviceIdType.MESH
F32 = jnp.float32
BF16 = jnp.bfloat16


def peer(me, i):
    y, x, z, c = me // 16, (me // 4) % 4, (me // 2) % 2, me % 2
    y = (y + i // 16) % 4
    x = (x + (i // 4) % 4) % 4
    z = (z + (i // 2) % 2) % 2
    c = (c + i % 2) % 2
    return ((y * 4 + x) * 2 + z) * 2 + c


def loop(lo, hi, f):
    def step(i, carry):
        f(i)
        return carry

    lax.fori_loop(lo, hi, step, 0)


def layer_kernel(
    tok_hbm, gain_hbm, rf_hbm, cf_hbm, up_hbm, down_hbm, out_hbm,
    tok, gain, rf, cf, up, down, up_t, filt, recv, mix, back, gated, stat, result,
    in_sem, rf_sem, gain_sem, fs_sem, fr_sem, bs_sem, br_sem, ss_sem, sr_sem, out_sem,
):
    me = lax.axis_index("seq")
    part = lax.axis_index("chan")

    def cols(j):
        return pl.ds(pl.multiple_of(j * W, W), W)

    def rf_copy(j):
        return pltpu.make_async_copy(rf_hbm.at[cols(j)], rf.at[cols(j)], rf_sem.at[j])

    def gain_copy(j):
        return pltpu.make_async_copy(gain_hbm.at[:, :, cols(j)], gain.at[j], gain_sem.at[j])

    def tok_copy(r):
        return pltpu.make_async_copy(tok_hbm.at[r], tok.at[r], in_sem.at[0])

    weights = [
        pltpu.make_async_copy(cf_hbm, cf, in_sem.at[1]),
        pltpu.make_async_copy(up_hbm, up, in_sem.at[2]),
        pltpu.make_async_copy(down_hbm, down, in_sem.at[3]),
    ]
    loop(0, ROWS, lambda r: tok_copy(r).start())

    def start_chunk(j):
        rf_copy(j).start()
        gain_copy(j).start()

    start_chunk(0)

    barrier = pltpu.get_barrier_semaphore()

    def greet(i):
        pl.semaphore_signal(barrier, inc=1, device_id=(peer(me, i), part), device_id_type=MESH)

    loop(1, PEERS, greet)
    for i in range(1, PARTS):
        pl.semaphore_signal(barrier, inc=1, device_id=(me, (part + i) % PARTS), device_id_type=MESH)

    i0 = lax.broadcasted_iota(jnp.int32, (128, 128), 0)
    i1 = lax.broadcasted_iota(jnp.int32, (128, 128), 1)
    to_chan = jnp.where(i1 == (i0 % 8) * 16 + i0 // 8, 1.0, 0.0).astype(BF16)
    to_rows = jnp.where(i1 == (i0 % 16) * 8 + i0 // 16, 1.0, 0.0).astype(BF16)
    filt_rows = filt.reshape(NCH * CH * ROWS, W)
    back_rows = back.reshape(NCH * CH * ROWS, W)

    def block(j, c):
        return pl.ds(pl.multiple_of(j * (CH * ROWS) + c * ROWS, 128), 128)

    def row_mix(j, plane):
        c0 = pl.multiple_of(plane * PCH, 16)
        lhs = tok[:, pl.ds(c0, PCH), :].reshape(ROWS * PCH, COLS)
        spun = lax.dot_general(lhs, rf[cols(j), :], (((1,), (1,)), ((), ())), preferred_element_type=F32)
        spun = spun.reshape(ROWS, PCH, W)
        own = (gain[j, :, pl.ds(c0, PCH), :].astype(F32) * spun).astype(BF16)
        for c in range(0, PCH, 16):
            piece = own[:, c : c + 16, :].reshape(128, W)
            filt_rows[block(j, c0 + c), :] = jnp.dot(to_chan, piece, preferred_element_type=F32).astype(BF16)

    def my_rows(d):
        return pl.ds(pl.multiple_of(d * ROWS, ROWS), ROWS)

    def send_filtered(j, lo, hi):
        def one(i):
            d = peer(me, i)
            pltpu.make_async_remote_copy(
                src_ref=filt.at[j, pl.ds(OWN * d, OWN)],
                dst_ref=recv.at[j, :, my_rows(me), :],
                send_sem=fs_sem.at[j],
                recv_sem=fr_sem.at[j],
                device_id=(d, part),
                device_id_type=MESH,
            ).start()

        loop(lo, hi, one)

    def keep_filtered(j):
        pltpu.make_async_copy(filt.at[j, pl.ds(OWN * me, OWN)], recv.at[j, :, my_rows(me), :], fr_sem.at[j]).start()

    def col_mix(j):
        pltpu.make_async_copy(recv.at[j], recv.at[j], fr_sem.at[j]).wait()
        rhs = jnp.concatenate([recv[j, c] for c in range(OWN)], axis=1)
        mixed = jnp.dot(cf[...], rhs, preferred_element_type=F32).astype(BF16)
        for c in range(OWN):
            mix[j, c] = mixed[:, c * W : (c + 1) * W]

    def send_mixed(j):
        def one(i):
            d = peer(me, i)
            pltpu.make_async_remote_copy(
                src_ref=mix.at[j, :, my_rows(d), :],
                dst_ref=back.at[j, pl.ds(OWN * me, OWN)],
                send_sem=bs_sem.at[j],
                recv_sem=br_sem.at[j],
                device_id=(d, part),
                device_id_type=MESH,
            ).start()

        loop(1, PEERS, one)
        pltpu.make_async_copy(mix.at[j, :, my_rows(me), :], back.at[j, pl.ds(OWN * me, OWN)], br_sem.at[j]).start()

    def gate(j):
        pltpu.make_async_copy(back.at[j], back.at[j], br_sem.at[j]).wait()
        slot = j % 2
        total = jnp.zeros((ROWS, W), F32)
        for c in range(0, CH, 16):
            mixed = jnp.dot(to_rows, back_rows[block(j, c), :], preferred_element_type=F32).reshape(ROWS, 16, W)
            src = tok[:, c : c + 16, cols(j)].astype(F32)
            value = src + mixed * jax.nn.sigmoid(src)
            gated[slot, :, c : c + 16, :] = value
            total = total + jnp.sum(value, axis=1)
        mean = total * (1.0 / CH)
        squares = jnp.zeros((ROWS, W), F32)
        for c in range(0, CH, 16):
            off = gated[slot, :, c : c + 16, :] - mean[:, None, :]
            squares = squares + jnp.sum(off * off, axis=1)
        stat[j, part, 0] = total
        stat[j, part, 1] = squares
        for i in range(1, PARTS):
            pltpu.make_async_remote_copy(
                src_ref=stat.at[j, part],
                dst_ref=stat.at[j, part],
                send_sem=ss_sem.at[j],
                recv_sem=sr_sem.at[j],
                device_id=(me, (part + i) % PARTS),
                device_id_type=MESH,
            ).start()

    def out_copy(j):
        return pltpu.make_async_copy(result.at[j], out_hbm.at[:, :, cols(j)], out_sem.at[j])

    def channel_mlp(j):
        three = stat.at[j, pl.ds(0, PARTS - 1)]
        pltpu.make_async_copy(three, three, sr_sem.at[j]).wait()
        slot = j % 2
        totals = [stat[j, p, 0] for p in range(PARTS)]
        mean = (totals[0] + totals[1] + totals[2] + totals[3]) * (1.0 / D)
        spread = jnp.zeros((ROWS, W), F32)
        for p in range(PARTS):
            off = totals[p] * (1.0 / CH) - mean
            spread = spread + (stat[j, p, 1] + CH * (off * off))
        scale = lax.rsqrt(spread * (1.0 / D) + 1e-05)
        for r0 in range(0, ROWS, 2):
            value = jnp.concatenate([gated[slot, r] for r in (r0, r0 + 1)], axis=1)
            m = jnp.concatenate([mean[r : r + 1] for r in (r0, r0 + 1)], axis=1)
            s = jnp.concatenate([scale[r : r + 1] for r in (r0, r0 + 1)], axis=1)
            normed = ((value - m) * s).astype(BF16)
            hidden = jax.nn.gelu(jnp.dot(up_t[...], normed, preferred_element_type=F32)).astype(BF16)
            final = (value + jnp.dot(down[...], hidden, preferred_element_type=F32)).astype(BF16)
            result[j, r0] = final[:, :W]
            result[j, r0 + 1] = final[:, W:]
        out_copy(j).start()

    pltpu.make_async_copy(tok_hbm, tok, in_sem.at[0]).wait()

    def plane_of(step):
        return (me // PLANE + step) % PLANES

    def first(j):
        rf_copy(j).wait()
        gain_copy(j).wait()
        row_mix(j, plane_of(0))

        @pl.when(j == 0)
        def _():
            pl.semaphore_wait(barrier, PEERS - 1 + PARTS - 1)
            loop(1, NCH, start_chunk)
            for copy in weights:
                copy.start()

        send_filtered(j, 1, PLANE)
        keep_filtered(j)

        def later(step):
            row_mix(j, plane_of(step))
            send_filtered(j, step * PLANE, step * PLANE + PLANE)

        loop(1, PLANES, later)

    loop(0, NCH, first)
    for copy in weights:
        copy.wait()
    up_t[...] = up[...].astype(F32).T.astype(BF16)

    def second(j):
        @pl.when(j < NCH)
        def _():
            col_mix(j)
            send_mixed(j)

        @pl.when(jnp.logical_and(j >= LAG, j < NCH + LAG))
        def _():
            gate(j - LAG)

        @pl.when(j > LAG)
        def _():
            channel_mlp(j - LAG - 1)

    loop(0, NCH + LAG + 1, second)

    def drain(j):
        rest = filt.at[j, pl.ds(0, CH - OWN)]
        pltpu.make_async_copy(rest, rest, fs_sem.at[j]).wait()
        pltpu.make_async_copy(rest, rest, bs_sem.at[j]).wait()
        three = stat.at[j, pl.ds(0, PARTS - 1)]
        pltpu.make_async_copy(three, three, ss_sem.at[j]).wait()
        out_copy(j).wait()

    loop(0, NCH, drain)


def body(tokens, filter_gain, row_factor, col_factor, up_weight, down_weight):
    dma = pltpu.SemaphoreType.DMA
    return pl.pallas_call(
        layer_kernel,
        name="mixer_layer",
        out_shape=jax.ShapeDtypeStruct((ROWS, CH, COLS), BF16),
        in_specs=[pl.BlockSpec(memory_space=pl.ANY)] * 6,
        out_specs=pl.BlockSpec(memory_space=pl.ANY),
        scratch_shapes=[
            pltpu.VMEM((ROWS, CH, COLS), BF16),
            pltpu.VMEM((NCH, ROWS, CH, W), BF16),
            pltpu.VMEM((COLS, COLS), BF16),
            pltpu.VMEM((GA, GA), BF16),
            pltpu.VMEM((CH, HID), BF16),
            pltpu.VMEM((CH, HID), BF16),
            pltpu.VMEM((HID, CH), BF16),
            pltpu.VMEM((NCH, CH, ROWS, W), BF16),
            pltpu.VMEM((NCH, OWN, GA, W), BF16),
            pltpu.VMEM((NCH, OWN, GA, W), BF16),
            pltpu.VMEM((NCH, CH, ROWS, W), BF16),
            pltpu.VMEM((2, ROWS, CH, W), F32),
            pltpu.VMEM((NCH, PARTS, 2, ROWS, W), F32),
            pltpu.VMEM((NCH, ROWS, CH, W), BF16),
            dma((4,)),
        ]
        + [dma((NCH,))] * 9,
        compiler_params=pltpu.CompilerParams(
            collective_id=0, has_side_effects=True, vmem_limit_bytes=60 * 2**20
        ),
    )(tokens, filter_gain, row_factor, col_factor, up_weight[0], down_weight[0])


def solution(mesh):
    return jax.shard_map(
        body,
        mesh=mesh,
        in_specs=(
            P("seq", "chan", None),
            P("seq", "chan", None),
            P(),
            P(),
            P("chan", None, None),
            P("chan", None, None),
        ),
        out_specs=P("seq", "chan", None),
        check_vma=False,
    )
```
